512 devices in a mesh: row: 4 (over x), col: 128 (over y, z, core).
Axes of the slice: x: 4, y: 4, z: 16, core: 2. Of those that a mesh axis runs over, the one named last changes fastest.
Arguments:
- a_matrix: bfloat16 [4096, 65536], P('row', 'col'), may hold values from -0.0234375 to 0.0234375
- omega: bfloat16 [96, 65536], P(None, 'col'), may hold values from -6 to 6
- col_scale: float32 [65536], P('col'), may hold values from 1 to 48
- cone_point: float32 [4096], P('row'), may hold values from -8 to 8, as said below
- cone_id: int32 [4096], P('row'), may hold values from 0 to 4095, as said below
- cone_kind: int32 [4096], P('row'), may hold values from 0 to 1, as said below
Outputs:
- q_basis: float32 [96, 65536], P(None, 'col')
- r_factor: float32 [96, 96], replicated
The draws below stay inside these ranges and needn't reach their ends.
Inputs may be any that keep to these rules, and one draw needn't show every extreme that they name: `cone_id`: rows of one cone are consecutive and share one id, the index of the cone's first row; every cone lies inside an aligned block of 4 rows; the last row is a cone of its own. `cone_kind`: 1 marks a second-order cone, 0 nonnegative entries; equal on all rows of a cone; 1 only on cones of two rows or more. `cone_point`: on a second-order cone every non-head entry has magnitude 0.5 or more, and the head's magnitude is at most 0.95 times the norm of the other entries.
All inputs are finite; a program needn't handle non-finite values.
Results may differ from the reference program's by a relative error of at most 0.014.
Values may be sent and summed in bfloat16 or wider, within the bound.
A program may use at most 64 MiB of HBM per device.

```python
import jax
import jax.numpy as jnp
from jax import lax

SKETCH = 96
COL_DEV = 512
R_DEV = 1024
CONE_SPAN = 4
PASSES = 2
VARS = 65536
ROWS = 4096
N_ROW = 4
N_COL = 128


def cone_layout(key):
    base = jax.random.fold_in(key, 7)
    first_key, second_key = jax.random.split(base)
    total = R_DEV * N_ROW
    positions = jnp.arange(total, dtype=jnp.int32)
    cuts = (jax.random.randint(first_key, (total,), 0, 3) == 0) | (positions % CONE_SPAN == 0) | (positions == total - 1)
    starts = lax.cummax(jnp.where(cuts, positions, 0), axis=0).astype(jnp.int32)
    cone_ids = starts
    sizes = jax.ops.segment_sum(jnp.ones((total,), jnp.int32), cone_ids, num_segments=total)[cone_ids]
    coin = jax.random.randint(second_key, (total,), 0, 2)
    kinds = jnp.where(sizes >= 2, coin[starts], 0).astype(jnp.int32)
    return (cone_ids, kinds, cuts)


def draw_cone_id(key, part):
    return cone_layout(key)[0]


def draw_cone_kind(key, part):
    return cone_layout(key)[1]


def draw_cone_point(key, part):
    cone_ids, kinds, cuts = cone_layout(key)
    total = R_DEV * N_ROW
    float_key = jax.random.fold_in(key, 11)
    mag_key, sign_key, head_key, drawn_key = jax.random.split(float_key, 4)
    signs = jnp.where(jax.random.randint(sign_key, (total,), 0, 2) == 0, -1.0, 1.0)
    magnitude = jax.random.uniform(mag_key, (total,), jnp.float32, 0.5, 2.0)
    share = jax.random.uniform(head_key, (total,), jnp.float32, -0.8, 0.8)
    drawn = jax.random.normal(drawn_key, (total,), jnp.float32)
    second_order = kinds == 1
    tail_vals = jnp.where(second_order & ~cuts, signs * magnitude, 0.0)
    tail_norm = jnp.sqrt(jax.ops.segment_sum(tail_vals * tail_vals, cone_ids, num_segments=total)[cone_ids])
    soc_vals = jnp.where(cuts, share * tail_norm, tail_vals)
    return jnp.where(second_order, soc_vals, drawn).astype(jnp.float32)


def draw_col_scale(key, part):
    total = COL_DEV * N_COL
    positions = jnp.arange(total).astype(jnp.float32)
    base = jnp.exp(jax.random.uniform(key, (total,), jnp.float32, 0.0, jnp.log(10.0)))
    return (base * (1.0 + 2.0 * positions / (total - 1))).astype(jnp.float32)


def steps_of(key, dims, cuts, low, high):
    level, own = 1.0, jax.random.fold_in(key, 6)
    for position, blocks in cuts:
        steps = jnp.exp(jax.random.uniform(jax.random.fold_in(own, position), (blocks,), jnp.float32, low / len(cuts), high / len(cuts)))
        level = level * jnp.repeat(steps, dims[position] // blocks).reshape([-1 if axis == position else 1 for axis in range(len(dims))])
    return level


def centred(own_key, dims, scale, bound, pieces=(), held_as=jnp.bfloat16):
    factor_of = steps_of(own_key, dims, pieces, -0.22, 0.18) if pieces else 1.0
    array = jax.random.normal(own_key, dims, jnp.float32) * scale * factor_of
    return jnp.minimum(jnp.maximum(array, -bound), bound).astype(held_as)


def setup_inputs(seed: int = 0) -> dict:
    key_of = jax.random.split(jax.random.key(seed), 7)
    a_matrix = centred(key_of[0], (ROWS, VARS), VARS ** -0.5, 0.0234375, ((0, 4), (1, 128)))
    omega = centred(key_of[1], (SKETCH, VARS), 1.0, 6.0, ((1, 128),))
    col_scale = draw_col_scale(jax.random.fold_in(key_of[6], 71), 0)
    cone_point = draw_cone_point(jax.random.fold_in(key_of[6], 71), 0)
    cone_id = draw_cone_id(jax.random.fold_in(key_of[6], 71), 0)
    cone_kind = draw_cone_kind(jax.random.fold_in(key_of[6], 71), 0)
    return {"a_matrix": a_matrix, "omega": omega, "col_scale": col_scale, "cone_point": cone_point, "cone_id": cone_id, "cone_kind": cone_kind}


def apply_cones(sketch_rows, cone_point, cone_id, cone_kind):
    total = cone_point.shape[0]
    values = sketch_rows.T
    previous = jnp.concatenate([cone_id[:1] - 1, cone_id[:-1]])
    is_head = cone_id != previous
    second_order = cone_kind == 1

    def segment(vals):
        return jax.ops.segment_sum(vals, cone_id, num_segments=total)[cone_id]
    tail_vals = jnp.where(second_order & ~is_head, cone_point, jnp.float32(0.0))
    tail_norm = jnp.sqrt(jnp.where(second_order, segment(tail_vals * tail_vals), jnp.float32(1.0)))
    head_val = segment(jnp.where(is_head, cone_point, jnp.float32(0.0)))
    cone_ratio = (head_val / tail_norm)[:, None]
    unit_tail = (tail_vals / tail_norm)[:, None]
    head_part = segment(jnp.where(is_head[:, None], values, jnp.float32(0.0)))
    projected = segment(unit_tail * values)
    soc_out = jnp.where(is_head[:, None], 0.5 * (head_part + projected), 0.5 * (unit_tail * head_part + (1.0 + cone_ratio) * values - cone_ratio * unit_tail * projected))
    positive = jnp.where(cone_point > 0, jnp.float32(1.0), jnp.float32(0.0))[:, None]
    result = jnp.where(second_order[:, None], soc_out, positive * values)
    return result.T

def reference(a_matrix, omega, col_scale, cone_point, cone_id, cone_kind):
    vectors = omega
    for repeat in range(PASSES):
        scaled = (vectors.astype(jnp.float32) * col_scale[None, :]).astype(jnp.bfloat16)
        sketch_rows = lax.dot_general(scaled.astype(jnp.float32), a_matrix.astype(jnp.float32), (((1,), (1,)), ((), ())), preferred_element_type=jnp.float32)
        weighted = apply_cones(sketch_rows, cone_point, cone_id, cone_kind).astype(jnp.bfloat16)
        back = jnp.dot(weighted.astype(jnp.float32), a_matrix.astype(jnp.float32), preferred_element_type=jnp.float32) * col_scale[None, :]
        gram_matrix = jnp.dot(back, back.T, precision=lax.Precision.HIGHEST) / VARS
        lower_factor = jnp.linalg.cholesky(gram_matrix)
        orth_basis = lax.linalg.triangular_solve(lower_factor, back, left_side=True, lower=True)
        vectors = orth_basis.astype(jnp.bfloat16)
    return (orth_basis, lower_factor.T)
```

```python
import jax
import jax.numpy as jnp
from jax import lax
from jax.experimental import pallas as pl
from jax.experimental.pallas import tpu as pltpu
from jax.sharding import Mesh
from jax.sharding import PartitionSpec as P

PASSES = 2
LANES = 128
SUB = 8
COL = ("col_0", "col_1", "col_2")
MESH = pl.DeviceIdType.MESH
HIGHEST = lax.Precision.HIGHEST
NT = (((1,), (1,)), ((), ()))


def offsets_far_first(n):
    return sorted(range(1, n), key=lambda r: -min(r, n - r))


def iota(dim, shape=(SUB, LANES)):
    return lax.broadcasted_iota(jnp.int32, shape, dim)


def factor_and_inverse(gram):
    n = gram.shape[0]
    blocks = n // SUB
    wide = jnp.concatenate([gram, jnp.zeros((n, LANES - n), jnp.float32)], axis=1)
    m = [wide[SUB * i : SUB * (i + 1)] for i in range(blocks)]
    lane, row = iota(1), iota(0)
    upper = [jnp.zeros((SUB, LANES), jnp.float32) for _ in range(blocks)]
    inverse = [jnp.zeros((SUB, LANES), jnp.float32) for _ in range(blocks)]

    def down(block, s):
        return jnp.broadcast_to(block[s : s + 1, :], (SUB, LANES))

    step = 4
    for j in range(0, n, step):
        jb, s0 = j // SUB, j % SUB
        cols = [
            {i: jnp.broadcast_to(m[i][:, j + t : j + t + 1], (SUB, LANES)) for i in range(jb, blocks)}
            for t in range(step)
        ]
        rows = [down(m[jb], s0 + t) for t in range(step)]
        mults, pivots = [], []
        for t in range(step):
            d = down(cols[t][jb], s0 + t)
            inv = 1.0 / d
            root = 1.0 / jnp.sqrt(d)
            at = row == s0 + t
            here = lane == j + t
            upper[jb] = jnp.where(at & (lane >= j + t), rows[t] * root, upper[jb])
            inverse[jb] = jnp.where(at & (lane < j + t), rows[t] * root, jnp.where(at & here, root, inverse[jb]))
            mult = {i: cols[t][i] * inv for i in cols[t]}
            pivot = jnp.where(here, 1.0, rows[t])
            for u in range(t + 1, step):
                rows[u] = jnp.where(here, 0.0, rows[u]) - down(mult[jb], s0 + u) * pivot
                head = down(cols[u][jb], s0 + t)
                cols[u] = {i: cols[u][i] - mult[i] * head for i in cols[u]}
            mults.append(mult)
            pivots.append(jnp.where((lane > j + t) & (lane < j + step), 0.0, pivot))
        inside = (lane >= j) & (lane < j + step)
        for i in range(jb, blocks):
            if i == jb and s0 + step == SUB:
                continue
            new = jnp.where(inside, 0.0, m[i])
            for t in range(step):
                new = new - mults[t][i] * pivots[t]
            m[i] = jnp.where(row >= s0 + step, new, m[i]) if i == jb else new
    return jnp.concatenate(upper, axis=0), jnp.concatenate(inverse, axis=0)


def cone_coefficients(point, ids, kinds):
    width = point.shape[1]

    def ahead(v, d):
        return v if d == 0 else pltpu.roll(v, (-d) % width, 1)

    is_head = jnp.where(ids != ahead(ids, -1), 1.0, 0.0)
    second = jnp.where(kinds == 1, 1.0, 0.0)
    tail = point * second * (1.0 - is_head)
    shifts = range(-3, 4)
    same = {d: jnp.where(ids == ahead(ids, d), 1.0, 0.0) for d in shifts}
    norm_sq = sum(same[d] * ahead(tail * tail, d) for d in shifts)
    head_value = sum(same[d] * ahead(point * is_head, d) for d in shifts)
    norm = jnp.sqrt(jnp.where(second > 0.5, norm_sq, 1.0))
    ratio = head_value / norm
    unit = tail / norm
    positive = jnp.where(point > 0, 1.0, 0.0)
    out = {}
    for d in shifts:
        eye = 1.0 if d == 0 else 0.0
        other_unit, other_head = ahead(unit, d), ahead(is_head, d)
        head_row = 0.5 * (eye + other_unit)
        tail_row = 0.5 * (unit * other_head + (1.0 + ratio) * eye - ratio * unit * other_unit)
        soc = same[d] * jnp.where(is_head > 0.5, head_row, tail_row)
        out[d] = jnp.where(second > 0.5, soc, positive * eye)
    return out


def kernel(
    sizes, omega_hbm, a_hbm, scale_hbm, point_hbm, id_hbm, kind_hbm, q_ref, r_ref,
    omega, a, scale, point, ids, kinds,
    part_out, part_in, cut_out, cut_in, gather_z, chunk_out, weighted, back_out, back_in,
    gram_out, gram_in, gram_z, gram_all,
    load_sem, s_part, r_part, s_cut, r_cut, s_gz, r_gz, s_w, r_w, s_x, r_x, s_ga, r_ga, s_gb, r_gb, s_gc, r_gc,
):
    nx, ny, nz, nc = sizes
    np_ = ny * nc
    sketch, variables = omega.shape
    rows_z = sketch // nz
    rows_p = sketch // np_
    total = variables * ny * nz * nc
    x, y, z, c = (lax.axis_index(n) for n in ("row",) + COL)
    p = y * nc + c

    def on_p(r):
        k = lax.rem(p + r, np_)
        return k, {"col_0": k // nc, "col_2": lax.rem(k, nc)}

    def on_z(r):
        k = lax.rem(z + r, nz)
        return k, {"col_1": k}

    def on_x(r):
        k = lax.rem(x + r, nx)
        return k, {"row": k}

    p_steps, z_steps, x_steps = offsets_far_first(np_), offsets_far_first(nz), offsets_far_first(nx)

    barrier = pltpu.get_barrier_semaphore()
    for on, steps in ((on_z, z_steps), (on_p, p_steps), (on_x, x_steps)):
        for r in steps:
            pl.semaphore_signal(barrier, inc=1, device_id=on(r)[1], device_id_type=MESH)

    loads = [
        pltpu.make_async_copy(src, dst, load_sem.at[k])
        for k, (src, dst) in enumerate(
            ((omega_hbm, omega), (scale_hbm, scale), (a_hbm, a), (point_hbm, point), (id_hbm, ids), (kind_hbm, kinds))
        )
    ]
    for copy in loads:
        copy.start()
    for copy in loads:
        copy.wait()

    def send(src, dst, ss, rs, where):
        copy = pltpu.make_async_remote_copy(
            src_ref=src, dst_ref=dst, send_sem=ss, recv_sem=rs, device_id=where, device_id_type=MESH
        )
        copy.start()
        return copy

    def arrive(dst, ss, rs, where):
        pltpu.make_async_remote_copy(
            src_ref=dst, dst_ref=dst, send_sem=ss, recv_sem=rs, device_id=where, device_id_type=MESH
        ).wait_recv()

    def drain(copies):
        for copy in copies:
            copy.wait_send()

    def sketch_part(scaled, k):
        block = a[pl.ds(pl.multiple_of(k * LANES, LANES), LANES), :]
        return lax.dot_general(scaled, block, NT, preferred_element_type=jnp.float32)

    pl.semaphore_wait(barrier, len(p_steps) + len(z_steps) + len(x_steps))

    coef = None
    pending = []
    scaled = (omega[...].astype(jnp.float32) * scale[...]).astype(jnp.bfloat16)
    first_back = None
    for g in range(PASSES):
        sends = []
        for r in p_steps:
            k, where = on_p(r)
            part_out[g, k] = sketch_part(scaled, k).astype(jnp.bfloat16)
            sends.append(send(part_out.at[g, k], part_in.at[g, p], s_part.at[g, r], r_part.at[g, p], where))
        owned = sketch_part(scaled, p)
        drain(pending)
        gram_sends = []
        if g == 1:
            gram_sends = gram_scatter(0)
        if coef is None:
            coef = cone_coefficients(point[pl.ds(p, 1), :], ids[pl.ds(p, 1), :], kinds[pl.ds(p, 1), :])
        for r in p_steps:
            k, where = on_p(r)
            arrive(part_in.at[g, k], s_part.at[g, r], r_part.at[g, k], where)
            owned = owned + part_in[g, k].astype(jnp.float32)
        for t in range(nz):
            cut_out[g, t] = owned[rows_z * t : rows_z * (t + 1), :].astype(jnp.bfloat16)
        cut_sends = []
        for r in z_steps:
            k, where = on_z(r)
            cut_sends.append(send(cut_out.at[g, k], cut_in.at[g, z], s_cut.at[g, r], r_cut.at[g, z], where))
        drain(sends)
        if g == 1:
            gram_sends = gram_sends + gram_cross(0)
        mine = cut_out[g, z].astype(jnp.float32)
        for r in z_steps[::-1]:
            k, where = on_z(r)
            arrive(cut_in.at[g, k], s_cut.at[g, r], r_cut.at[g, k], where)
            mine = mine + cut_in[g, k].astype(jnp.float32)
        shaped = sum(
            coef[d] * (mine if d == 0 else pltpu.roll(mine, (-d) % LANES, 1)) for d in range(-3, 4)
        )
        gather_z[g, z] = shaped.astype(jnp.bfloat16)
        z_sends = []
        for r in z_steps:
            k, where = on_z(r)
            z_sends.append(send(gather_z.at[g, z], gather_z.at[g, z], s_gz.at[g, r], r_gz.at[g, z], where))
        drain(cut_sends)
        if g == 1:
            gram_sends = gram_sends + gram_spread(0)
        for r in z_steps[::-1]:
            k, where = on_z(r)
            arrive(gather_z.at[g, k], s_gz.at[g, r], r_gz.at[g, k], where)
        chunk = jnp.concatenate([gather_z[g, t].astype(jnp.float32) for t in range(nz)], axis=0).astype(jnp.bfloat16)
        chunk_out[g] = chunk
        w_sends = []
        for r in p_steps:
            k, where = on_p(r)
            w_sends.append(send(chunk_out.at[g], weighted.at[g, p], s_w.at[g, r], r_w.at[g, p], where))
        weighted[g, p] = chunk
        drain(z_sends)
        for r in p_steps:
            k, where = on_p(r)
            arrive(weighted.at[g, k], s_w.at[g, r], r_w.at[g, k], where)
        whole = jnp.concatenate([weighted[g, t] for t in range(np_)], axis=1)
        back = jnp.dot(whole, a[...], preferred_element_type=jnp.float32).astype(jnp.bfloat16)
        back_out[g] = back
        x_sends = []
        for r in x_steps:
            k, where = on_x(r)
            x_sends.append(send(back_out.at[g], back_in.at[g, x], s_x.at[g, r], r_x.at[g, x], where))
        back_in[g, x] = back
        drain(w_sends)
        if g == 1:
            gram = gram_collect(0)
            drain(gram_sends)
            _, inverse = factor_and_inverse(gram)
        for r in x_steps:
            k, where = on_x(r)
            arrive(back_in.at[g, k], s_x.at[g, r], r_x.at[g, k], where)
        pending = x_sends
        summed = back_in[g, 0].astype(jnp.float32)
        for t in range(1, nx):
            summed = summed + back_in[g, t].astype(jnp.float32)
        summed = summed * scale[...]

        def gram_scatter(h):
            local = gram_local[0]
            for t in range(np_):
                gram_out[h, t] = local[rows_p * t : rows_p * (t + 1), :]
            out = []
            for r in p_steps:
                k, where = on_p(r)
                out.append(send(gram_out.at[h, k], gram_in.at[h, p], s_ga.at[h, r], r_ga.at[h, p], where))
            gram_in[h, p] = gram_out[h, p]
            return out

        def gram_cross(h):
            for r in p_steps:
                k, where = on_p(r)
                arrive(gram_in.at[h, k], s_ga.at[h, r], r_ga.at[h, k], where)
            gram_z[h, z] = jnp.sum(gram_in[h], axis=0)
            out = []
            for r in z_steps:
                k, where = on_z(r)
                out.append(send(gram_z.at[h, z], gram_z.at[h, z], s_gb.at[h, r], r_gb.at[h, z], where))
            return out

        def gram_spread(h):
            for r in z_steps[::-1]:
                k, where = on_z(r)
                arrive(gram_z.at[h, k], s_gb.at[h, r], r_gb.at[h, k], where)
            gram_all[h, p] = jnp.sum(gram_z[h], axis=0) / total
            out = []
            for r in p_steps:
                k, where = on_p(r)
                out.append(send(gram_all.at[h, p], gram_all.at[h, p], s_gc.at[h, r], r_gc.at[h, p], where))
            return out

        def gram_collect(h):
            for r in p_steps:
                k, where = on_p(r)
                arrive(gram_all.at[h, k], s_gc.at[h, r], r_gc.at[h, k], where)
            return jnp.concatenate([gram_all[h, t] for t in range(np_)], axis=0)

        if g == 0:
            gram_local = [lax.dot_general(summed, summed, NT, precision=HIGHEST, preferred_element_type=jnp.float32)]
            scaled = (summed * scale[...]).astype(jnp.bfloat16)
        else:
            final = jnp.dot(inverse[:, :sketch], summed, precision=HIGHEST, preferred_element_type=jnp.float32)
            gram_local = [lax.dot_general(final, final, NT, precision=HIGHEST, preferred_element_type=jnp.float32)]
            sends = gram_scatter(1)
            drain(pending)
            sends = sends + gram_cross(1) + gram_spread(1)
            upper, inverse = factor_and_inverse(gram_collect(1))
            q_ref[...] = jnp.dot(inverse[:, :sketch], final, precision=HIGHEST, preferred_element_type=jnp.float32)
            r_ref[...] = upper[:, :sketch]
            drain(sends)


def local(a_matrix, omega, col_scale, cone_point, cone_id, cone_kind):
    sketch, variables = omega.shape
    rows = a_matrix.shape[0]
    nx, ny, nz, nc = (lax.axis_size(n) for n in ("row",) + COL)
    np_ = ny * nc
    g = PASSES
    bf, f32 = jnp.bfloat16, jnp.float32
    dma = pltpu.SemaphoreType.DMA
    any_spec = pl.BlockSpec(memory_space=pl.ANY)
    vmem_spec = pl.BlockSpec(memory_space=pltpu.VMEM)
    per_p, per_z, per_x = dma((g, np_)), dma((g, nz)), dma((g, nx))

    def body(*refs):
        kernel((nx, ny, nz, nc), *refs)

    return tuple(
        pl.pallas_call(
            body,
            out_shape=(
                jax.ShapeDtypeStruct((sketch, variables), f32),
                jax.ShapeDtypeStruct((sketch, sketch), f32),
            ),
            in_specs=[any_spec] * 6,
            out_specs=(vmem_spec, vmem_spec),
            scratch_shapes=[
                pltpu.VMEM((sketch, variables), bf),
                pltpu.VMEM((rows, variables), bf),
                pltpu.VMEM((1, variables), f32),
                pltpu.VMEM((np_, LANES), f32),
                pltpu.VMEM((np_, LANES), jnp.int32),
                pltpu.VMEM((np_, LANES), jnp.int32),
                pltpu.VMEM((g, np_, sketch, LANES), bf),
                pltpu.VMEM((g, np_, sketch, LANES), bf),
                pltpu.VMEM((g, nz, sketch // nz, LANES), bf),
                pltpu.VMEM((g, nz, sketch // nz, LANES), bf),
                pltpu.VMEM((g, nz, sketch // nz, LANES), bf),
                pltpu.VMEM((g, sketch, LANES), bf),
                pltpu.VMEM((g, np_, sketch, LANES), bf),
                pltpu.VMEM((g, sketch, variables), bf),
                pltpu.VMEM((g, nx, sketch, variables), bf),
                pltpu.VMEM((g, np_, sketch // np_, sketch), f32),
                pltpu.VMEM((g, np_, sketch // np_, sketch), f32),
                pltpu.VMEM((g, nz, sketch // np_, sketch), f32),
                pltpu.VMEM((g, np_, sketch // np_, sketch), f32),
                dma((6,)),
                per_p, per_p, per_z, per_z, per_z, per_z, per_p, per_p, per_x, per_x,
                per_p, per_p, per_z, per_z, per_p, per_p,
            ],
            compiler_params=pltpu.CompilerParams(collective_id=0, has_side_effects=True),
        )(
            omega,
            a_matrix,
            col_scale.reshape(1, variables),
            cone_point.reshape(np_, LANES),
            cone_id.reshape(np_, LANES),
            cone_kind.reshape(np_, LANES),
        )
    )


def solution(mesh):
    shape = mesh.shape
    parts = (4, 16, 2) if shape["col"] == 128 else (1, shape["col"], 1)
    split = Mesh(mesh.devices.reshape(shape["row"], *parts), ("row",) + COL)
    in_specs = (P("row", COL), P(None, COL), P(COL), P("row"), P("row"), P("row"))
    out_specs = (P(None, COL), P())
    return jax.shard_map(local, mesh=split, in_specs=in_specs, out_specs=out_specs, check_vma=False)
```

```python
import jax
import jax.numpy as jnp
from jax import lax
from jax.experimental import pallas as pl
from jax.experimental.pallas import tpu as pltpu
from jax.sharding import Mesh
from jax.sharding import PartitionSpec as P

PASSES = 2
LANES = 128
SUB = 8
COL = ("col_0", "col_1", "col_2")
MESH = pl.DeviceIdType.MESH
HIGHEST = lax.Precision.HIGHEST
NT = (((1,), (1,)), ((), ()))


def offsets_far_first(n):
    return sorted(range(1, n), key=lambda r: -min(r, n - r))


def iota(dim, shape=(SUB, LANES)):
    return lax.broadcasted_iota(jnp.int32, shape, dim)


class Factor:
    STEP = 4

    def __init__(self, gram):
        self.n = n = gram.shape[0]
        self.blocks = n // SUB
        wide = jnp.concatenate([gram, jnp.zeros((n, LANES - n), jnp.float32)], axis=1)
        self.m = [wide[SUB * i : SUB * (i + 1)] for i in range(self.blocks)]
        self.upper = [jnp.zeros((SUB, LANES), jnp.float32) for _ in range(self.blocks)]
        self.inverse = [jnp.zeros((SUB, LANES), jnp.float32) for _ in range(self.blocks)]

    def run(self, first, last):
        m, upper, inverse, blocks, step = self.m, self.upper, self.inverse, self.blocks, self.STEP
        lane, row = iota(1), iota(0)

        def down(block, s):
            return jnp.broadcast_to(block[s : s + 1, :], (SUB, LANES))

        for j in range(first, last, step):
            jb, s0 = j // SUB, j % SUB
            cols = [
                {i: jnp.broadcast_to(m[i][:, j + t : j + t + 1], (SUB, LANES)) for i in range(jb, blocks)}
                for t in range(step)
            ]
            rows = [down(m[jb], s0 + t) for t in range(step)]
            mults, pivots = [], []
            for t in range(step):
                d = down(cols[t][jb], s0 + t)
                inv = 1.0 / d
                root = 1.0 / jnp.sqrt(d)
                at = row == s0 + t
                here = lane == j + t
                upper[jb] = jnp.where(at & (lane >= j + t), rows[t] * root, upper[jb])
                inverse[jb] = jnp.where(at & (lane < j + t), rows[t] * root, jnp.where(at & here, root, inverse[jb]))
                mult = {i: cols[t][i] * inv for i in cols[t]}
                pivot = jnp.where(here, 1.0, rows[t])
                for u in range(t + 1, step):
                    rows[u] = jnp.where(here, 0.0, rows[u]) - down(mult[jb], s0 + u) * pivot
                    head = down(cols[u][jb], s0 + t)
                    cols[u] = {i: cols[u][i] - mult[i] * head for i in cols[u]}
                mults.append(mult)
                pivots.append(jnp.where((lane > j + t) & (lane < j + step), 0.0, pivot))
            inside = (lane >= j) & (lane < j + step)
            for i in range(jb, blocks):
                if i == jb and s0 + step == SUB:
                    continue
                new = jnp.where(inside, 0.0, m[i])
                for t in range(step):
                    new = new - mults[t][i] * pivots[t]
                m[i] = jnp.where(row >= s0 + step, new, m[i]) if i == jb else new

    def result(self):
        return jnp.concatenate(self.upper, axis=0), jnp.concatenate(self.inverse, axis=0)


def cone_coefficients(point, ids, kinds):
    width = point.shape[1]

    def ahead(v, d):
        return v if d == 0 else pltpu.roll(v, (-d) % width, 1)

    is_head = jnp.where(ids != ahead(ids, -1), 1.0, 0.0)
    second = jnp.where(kinds == 1, 1.0, 0.0)
    tail = point * second * (1.0 - is_head)
    shifts = range(-3, 4)
    same = {d: jnp.where(ids == ahead(ids, d), 1.0, 0.0) for d in shifts}
    norm_sq = sum(same[d] * ahead(tail * tail, d) for d in shifts)
    head_value = sum(same[d] * ahead(point * is_head, d) for d in shifts)
    norm = jnp.sqrt(jnp.where(second > 0.5, norm_sq, 1.0))
    ratio = head_value / norm
    unit = tail / norm
    positive = jnp.where(point > 0, 1.0, 0.0)
    out = {}
    for d in shifts:
        eye = 1.0 if d == 0 else 0.0
        other_unit, other_head = ahead(unit, d), ahead(is_head, d)
        head_row = 0.5 * (eye + other_unit)
        tail_row = 0.5 * (unit * other_head + (1.0 + ratio) * eye - ratio * unit * other_unit)
        soc = same[d] * jnp.where(is_head > 0.5, head_row, tail_row)
        out[d] = jnp.where(second > 0.5, soc, positive * eye)
    return out


def kernel(
    sizes, omega_hbm, a_hbm, scale_hbm, point_hbm, id_hbm, kind_hbm, q_ref, r_ref,
    omega, a, scale, point, ids, kinds,
    part_out, part_in, cut, weighted, near_out, near_in, far_out, far_in,
    gram_out, gram_in, gram_z, gram_all,
    load_sem, a_sem, relay_sem,
    s_part, r_part, s_cut, r_cut, s_w, r_w, s_near, r_near, s_far, r_far, s_ga, r_ga, s_gb, r_gb, s_gc, r_gc,
):
    nx, ny, nz, nc = sizes
    np_ = ny * nc
    ng, nh = 2 * np_, nz // 2
    sketch, variables = omega.shape
    half_k, half_n = sketch // 2, variables // 2
    rows_g = sketch // ng
    total = variables * ny * nz * nc
    x, y, z, c = (lax.axis_index(n) for n in ("row",) + COL)
    p = y * nc + c
    zh, zl = z // 2, lax.rem(z, 2)
    h = p * 2 + zl

    def member(k):
        q = k // 2
        return {"col_0": q // nc, "col_1": zh * 2 + lax.rem(k, 2), "col_2": lax.rem(q, nc)}

    def on_g(r):
        k = lax.rem(h + r, ng)
        return k, member(k)

    def on_h(r):
        k = lax.rem(zh + r, nh)
        return k, {"col_1": k * 2 + zl}

    partners = [{"row": x + 1 - 2 * lax.rem(x, 2)}, {"row": 3 - x}] if nx == 4 else []
    p_steps, g_steps, h_steps = offsets_far_first(np_), offsets_far_first(ng), offsets_far_first(nh)
    near_h = sorted({1, nh - 1}) if nh > 1 else []

    barrier = pltpu.get_barrier_semaphore()
    greet = [on_g(r)[1] for r in g_steps] + [on_h(r)[1] for r in near_h] + partners
    for where in greet:
        pl.semaphore_signal(barrier, inc=1, device_id=where, device_id_type=MESH)

    def a_rows(k):
        return pl.ds(pl.multiple_of(k * LANES, LANES), LANES)

    def load_a(k):
        return pltpu.make_async_copy(a_hbm.at[a_rows(k), :], a.at[a_rows(k), :], a_sem.at[k])

    loads = [
        pltpu.make_async_copy(src, dst, load_sem.at[k])
        for k, (src, dst) in enumerate(
            ((omega_hbm, omega), (scale_hbm, scale), (point_hbm, point), (id_hbm, ids), (kind_hbm, kinds))
        )
    ]
    for copy in loads[:2]:
        copy.start()
    for r in p_steps + [0]:
        load_a(lax.rem(p + r, np_)).start()
    for copy in loads[2:]:
        copy.start()

    def send(src, dst, ss, rs, where):
        copy = pltpu.make_async_remote_copy(
            src_ref=src, dst_ref=dst, send_sem=ss, recv_sem=rs, device_id=where, device_id_type=MESH
        )
        copy.start()
        return copy

    def arrive(dst, ss, rs, where):
        pltpu.make_async_remote_copy(
            src_ref=dst, dst_ref=dst, send_sem=ss, recv_sem=rs, device_id=where, device_id_type=MESH
        ).wait_recv()

    def drain(copies):
        for copy in copies:
            copy.wait_send()

    def sketch_part(scaled, k):
        return lax.dot_general(scaled, a[a_rows(k), :], NT, preferred_element_type=jnp.float32)

    def add_up(ref, g, count):
        out = ref[g, 0].astype(jnp.float32)
        for t in range(1, count):
            out = out + ref[g, t].astype(jnp.float32)
        return out

    def gram_scatter(g, rows):
        local = lax.dot_general(rows, rows, NT, precision=HIGHEST, preferred_element_type=jnp.float32)
        for t in range(ng):
            gram_out[g, t] = local[rows_g * t : rows_g * (t + 1), :]
        out = []
        for r in g_steps:
            k, where = on_g(r)
            out.append(send(gram_out.at[g, k], gram_in.at[g, h], s_ga.at[g, r], r_ga.at[g, h], where))
        gram_in[g, h] = gram_out[g, h]
        return out

    def gram_cross(g):
        for r in g_steps:
            k, where = on_g(r)
            arrive(gram_in.at[g, k], s_ga.at[g, r], r_ga.at[g, k], where)
        gram_z[g, zh] = add_up(gram_in, g, ng)
        out = []
        for r in h_steps:
            k, where = on_h(r)
            out.append(send(gram_z.at[g, zh], gram_z.at[g, zh], s_gb.at[g, r], r_gb.at[g, zh], where))
        return out

    def gram_spread(g):
        for r in h_steps[::-1]:
            k, where = on_h(r)
            arrive(gram_z.at[g, k], s_gb.at[g, r], r_gb.at[g, k], where)
        gram_all[g, h] = add_up(gram_z, g, nh) / total
        out = []
        for r in g_steps:
            k, where = on_g(r)
            out.append(send(gram_all.at[g, h], gram_all.at[g, h], s_gc.at[g, r], r_gc.at[g, h], where))
        return out

    def gram_collect(g):
        for r in g_steps:
            k, where = on_g(r)
            arrive(gram_all.at[g, k], s_gc.at[g, r], r_gc.at[g, k], where)
        return Factor(jnp.concatenate([gram_all[g, t] for t in range(ng)], axis=0))

    pl.semaphore_wait(barrier, len(greet))
    relays = []
    known = 1
    while known < nh // 2:
        relays.append(known)
        known *= 2

    def relay_signal(step):
        for side, r in enumerate((relays[step], nh - relays[step])):
            pl.semaphore_signal(relay_sem.at[step, side], inc=1, device_id=on_h(r)[1], device_id_type=MESH)

    def relay_wait(step):
        for side in range(2):
            pl.semaphore_wait(relay_sem.at[step, side], 1)

    if relays:
        relay_signal(0)
    for copy in loads[:2]:
        copy.wait()
    scaled = (omega[...].astype(jnp.float32) * scale[...]).astype(jnp.bfloat16)
    coef = None
    pending = []
    factor = None
    for g in range(PASSES):
        sends = []
        for r in p_steps + [0]:
            k = lax.rem(p + r, np_)
            if g == 0:
                load_a(k).wait()
            part = sketch_part(scaled, k)
            for t in range(2):
                part_out[g, k, t] = part[half_k * t : half_k * (t + 1)].astype(jnp.bfloat16)
            if r:
                for t in range(2):
                    to = 2 * k + t
                    sends.append(
                        send(part_out.at[g, k, t], part_in.at[g, h], s_part.at[g, to], r_part.at[g, h], member(to))
                    )
            else:
                to = 2 * p + 1 - zl
                sends.append(
                    send(part_out.at[g, p, 1 - zl], part_in.at[g, h], s_part.at[g, to], r_part.at[g, h], member(to))
                )
                owned = jnp.where(zl == 0, part[:half_k], part[half_k:])
        drain(pending)
        gram_sends = []
        if g == 0:
            for step in range(len(relays)):
                relay_wait(step)
                if step + 1 < len(relays):
                    relay_signal(step + 1)
            for copy in loads[2:]:
                copy.wait()
            coef = cone_coefficients(point[pl.ds(p, 1), :], ids[pl.ds(p, 1), :], kinds[pl.ds(p, 1), :])
        else:
            gram_sends = gram_scatter(0, summed)
        for r in g_steps:
            k, where = on_g(r)
            arrive(part_in.at[g, k], s_part.at[g, k], r_part.at[g, k], where)
            owned = owned + part_in[g, k].astype(jnp.float32)
        cut[g, zh] = owned.astype(jnp.bfloat16)
        cut_sends = []
        for r in h_steps:
            k, where = on_h(r)
            cut_sends.append(send(cut.at[g, zh], cut.at[g, zh], s_cut.at[g, r], r_cut.at[g, zh], where))
        drain(sends)
        if g == 1:
            gram_sends = gram_sends + gram_cross(0)
        for r in h_steps[::-1]:
            k, where = on_h(r)
            arrive(cut.at[g, k], s_cut.at[g, r], r_cut.at[g, k], where)
        mine = add_up(cut, g, nh)
        shaped = sum(coef[d] * (mine if d == 0 else pltpu.roll(mine, (-d) % LANES, 1)) for d in range(-3, 4))
        weighted[g, h] = shaped.astype(jnp.bfloat16)
        w_sends = []
        for r in g_steps:
            k, where = on_g(r)
            w_sends.append(send(weighted.at[g, h], weighted.at[g, h], s_w.at[g, r], r_w.at[g, h], where))
        drain(cut_sends)
        if g == 1:
            gram_sends = gram_sends + gram_spread(0)
        for r in g_steps:
            k, where = on_g(r)
            arrive(weighted.at[g, k], s_w.at[g, r], r_w.at[g, k], where)
        whole = jnp.concatenate(
            [jnp.concatenate([weighted[g, 2 * t], weighted[g, 2 * t + 1]], axis=0) for t in range(np_)], axis=1
        )
        near_sends, far_sends = [], []
        for t in range(2):
            back = jnp.dot(whole, a[:, half_n * t : half_n * (t + 1)], preferred_element_type=jnp.float32)
            near_out[g, t] = back.astype(jnp.bfloat16)
            if partners:
                near_sends.append(
                    send(near_out.at[g, t], near_in.at[g, t], s_near.at[g, t], r_near.at[g, t], partners[t])
                )
        drain(w_sends)
        if g == 1:
            factor = gram_collect(0)
            factor.run(0, half_k)
            drain(gram_sends)
        halves = []
        for t in range(2 if partners else 0):
            arrive(near_in.at[g, t], s_near.at[g, t], r_near.at[g, t], partners[t])
            pair = near_out[g, t].astype(jnp.float32) + near_in[g, t].astype(jnp.float32)
            far_out[g, t] = pair.astype(jnp.bfloat16)
            far_sends.append(
                send(far_out.at[g, t], far_in.at[g, t], s_far.at[g, t], r_far.at[g, t], partners[1 - t])
            )
        if g == 1:
            factor.run(half_k, sketch)
        for t in range(2):
            if partners:
                arrive(far_in.at[g, t], s_far.at[g, t], r_far.at[g, t], partners[1 - t])
                halves.append(far_out[g, t].astype(jnp.float32) + far_in[g, t].astype(jnp.float32))
            else:
                halves.append(near_out[g, t].astype(jnp.float32))
        pending = near_sends + far_sends
        summed = jnp.concatenate(halves, axis=1) * scale[...]
        if g == 0:
            scaled = (summed * scale[...]).astype(jnp.bfloat16)
        else:
            _, inverse = factor.result()
            final = jnp.dot(inverse[:, :sketch], summed, precision=HIGHEST, preferred_element_type=jnp.float32)
            sends = gram_scatter(1, final)
            drain(pending)
            sends = sends + gram_cross(1)
            sends = sends + gram_spread(1)
            factor = gram_collect(1)
            factor.run(0, sketch)
            upper, inverse = factor.result()
            q_ref[...] = jnp.dot(inverse[:, :sketch], final, precision=HIGHEST, preferred_element_type=jnp.float32)
            r_ref[...] = upper[:, :sketch]
            drain(sends)


def local(a_matrix, omega, col_scale, cone_point, cone_id, cone_kind):
    sketch, variables = omega.shape
    rows = a_matrix.shape[0]
    nx, ny, nz, nc = (lax.axis_size(n) for n in ("row",) + COL)
    np_ = ny * nc
    ng, nh = 2 * np_, nz // 2
    g = PASSES
    bf, f32, i32 = jnp.bfloat16, jnp.float32, jnp.int32
    dma = pltpu.SemaphoreType.DMA
    any_spec = pl.BlockSpec(memory_space=pl.ANY)
    vmem_spec = pl.BlockSpec(memory_space=pltpu.VMEM)
    per_g, per_h, per_x = dma((g, ng)), dma((g, nh)), dma((g, 2))
    cross = pltpu.VMEM((g, 2, sketch, variables // 2), bf)

    def body(*refs):
        kernel((nx, ny, nz, nc), *refs)

    return tuple(
        pl.pallas_call(
            body,
            out_shape=(
                jax.ShapeDtypeStruct((sketch, variables), f32),
                jax.ShapeDtypeStruct((sketch, sketch), f32),
            ),
            in_specs=[any_spec] * 6,
            out_specs=(vmem_spec, vmem_spec),
            scratch_shapes=[
                pltpu.VMEM((sketch, variables), bf),
                pltpu.VMEM((rows, variables), bf),
                pltpu.VMEM((1, variables), f32),
                pltpu.VMEM((np_, LANES), f32),
                pltpu.VMEM((np_, LANES), i32),
                pltpu.VMEM((np_, LANES), i32),
                pltpu.VMEM((g, np_, 2, sketch // 2, LANES), bf),
                pltpu.VMEM((g, ng, sketch // 2, LANES), bf),
                pltpu.VMEM((g, nh, sketch // 2, LANES), bf),
                pltpu.VMEM((g, ng, sketch // 2, LANES), bf),
                cross, cross, cross, cross,
                pltpu.VMEM((g, ng, sketch // ng, sketch), f32),
                pltpu.VMEM((g, ng, sketch // ng, sketch), f32),
                pltpu.VMEM((g, nh, sketch // ng, sketch), f32),
                pltpu.VMEM((g, ng, sketch // ng, sketch), f32),
                dma((5,)),
                dma((np_,)),
                pltpu.SemaphoreType.REGULAR((3, 2)),
                per_g, per_g, per_h, per_h, per_g, per_g, per_x, per_x, per_x, per_x,
                per_g, per_g, per_h, per_h, per_g, per_g,
            ],
            compiler_params=pltpu.CompilerParams(collective_id=0, has_side_effects=True),
        )(
            omega,
            a_matrix,
            col_scale.reshape(1, variables),
            cone_point.reshape(np_, LANES),
            cone_id.reshape(np_, LANES),
            cone_kind.reshape(np_, LANES),
        )
    )


def solution(mesh):
    shape = mesh.shape
    parts = (4, 16, 2) if shape["col"] == 128 else (1, shape["col"], 1)
    split = Mesh(mesh.devices.reshape(shape["row"], *parts), ("row",) + COL)
    in_specs = (P("row", COL), P(None, COL), P(COL), P("row"), P("row"), P("row"))
    out_specs = (P(None, COL), P())
    return jax.shard_map(local, mesh=split, in_specs=in_specs, out_specs=out_specs, check_vma=False)
```

```python
import jax
import jax.numpy as jnp
from jax import lax
from jax.experimental import pallas as pl
from jax.experimental.pallas import tpu as pltpu
from jax.sharding import Mesh
from jax.sharding import PartitionSpec as P

PASSES = 2
PIECES = ((0, 16), (16, 32))
LANES = 128
SUB = 8
COL = ("col_0", "col_1", "col_2")
MESH = pl.DeviceIdType.MESH
NT = (((1,), (1,)), ((), ()))


def offsets_far_first(n):
    return sorted(range(1, n), key=lambda r: -min(r, n - r))


def iota(dim, shape=(SUB, LANES)):
    return lax.broadcasted_iota(jnp.int32, shape, dim)


class Factor:
    STEP = 8

    def __init__(self, gram):
        self.n = n = gram.shape[0]
        self.blocks = n // SUB
        self.m = [gram[SUB * i : SUB * (i + 1)] for i in range(self.blocks)]
        self.upper = [jnp.zeros((SUB, LANES), jnp.float32) for _ in range(self.blocks)]
        self.inverse = [jnp.zeros((SUB, LANES), jnp.float32) for _ in range(self.blocks)]

    def run(self, first, last):
        m, upper, inverse, blocks, step = self.m, self.upper, self.inverse, self.blocks, self.STEP
        lane, row = iota(1), iota(0)

        def down(block, s):
            return jnp.broadcast_to(block[s : s + 1, :], (SUB, LANES))

        for j in range(first, last, step):
            jb, s0 = j // SUB, j % SUB
            cols = [
                {i: jnp.broadcast_to(m[i][:, j + t : j + t + 1], (SUB, LANES)) for i in range(jb, blocks)}
                for t in range(step)
            ]
            rows = [down(m[jb], s0 + t) for t in range(step)]
            mults, pivots = [], []
            for t in range(step):
                d = down(cols[t][jb], s0 + t)
                inv = 1.0 / d
                root = lax.rsqrt(d)
                at = row == s0 + t
                here = lane == j + t
                upper[jb] = jnp.where(at & (lane >= j + t), rows[t] * root, upper[jb])
                inverse[jb] = jnp.where(at & (lane < j + t), rows[t] * root, jnp.where(at & here, root, inverse[jb]))
                mult = {i: cols[t][i] * inv for i in cols[t]}
                pivot = jnp.where(here, 1.0, rows[t])
                for u in range(t + 1, step):
                    rows[u] = jnp.where(here, 0.0, rows[u]) - down(mult[jb], s0 + u) * pivot
                    head = down(cols[u][jb], s0 + t)
                    cols[u] = {i: cols[u][i] - mult[i] * head for i in cols[u]}
                mults.append(mult)
                pivots.append(jnp.where((lane > j + t) & (lane < j + step), 0.0, pivot))
            inside = (lane >= j) & (lane < j + step)
            for i in range(jb, blocks):
                if i == jb and s0 + step == SUB:
                    continue
                new = jnp.where(inside, 0.0, m[i])
                for t in range(step):
                    new = new - mults[t][i] * pivots[t]
                m[i] = jnp.where(row >= s0 + step, new, m[i]) if i == jb else new

    def result(self):
        return jnp.concatenate(self.upper, axis=0), jnp.concatenate(self.inverse, axis=0)


def split_dot(left, right):
    f32, bf = jnp.float32, jnp.bfloat16
    lh, rh = left.astype(bf), right.astype(bf)
    ll, rl = (left - lh.astype(f32)).astype(bf), (right - rh.astype(f32)).astype(bf)
    small = jnp.dot(ll, rh, preferred_element_type=f32) + jnp.dot(lh, rl, preferred_element_type=f32)
    return jnp.dot(lh, rh, preferred_element_type=f32) + small


def packed(gram):
    n = gram.shape[0]
    wide = jnp.concatenate([gram, jnp.zeros((n, LANES - n), jnp.float32)], axis=1)
    tiles = [wide[SUB * i : SUB * (i + 1)] for i in range(n // SUB)]
    lane = iota(1)
    out = []
    for i in range(n // SUB // 2):
        cut = SUB * (i + 1)
        out.append(jnp.where(lane < cut, tiles[i], pltpu.roll(tiles[-1 - i], cut, 1)))
    return jnp.concatenate(out, axis=0)


def unpacked(half):
    count = half.shape[0] // SUB
    lane = iota(1)
    low, high = [], []
    for i in range(count):
        tile = half[SUB * i : SUB * (i + 1)]
        cut = SUB * (i + 1)
        low.append(jnp.where(lane < cut, tile, 0.0))
        high.append(jnp.where(lane < SUB * (2 * count - i), pltpu.roll(tile, LANES - cut, 1), 0.0))
    n = 2 * count * SUB
    lower = jnp.concatenate(low + high[::-1] + [jnp.zeros((LANES - n, LANES), jnp.float32)], axis=0)
    row, col = iota(0, (LANES, LANES)), iota(1, (LANES, LANES))
    return jnp.where(col // SUB > row // SUB, lower.T, lower)[:n]


def cone_coefficients(point, ids, kinds):
    width = point.shape[1]

    def ahead(v, d):
        return v if d == 0 else pltpu.roll(v, (-d) % width, 1)

    is_head = jnp.where(ids != ahead(ids, -1), 1.0, 0.0)
    second = jnp.where(kinds == 1, 1.0, 0.0)
    tail = point * second * (1.0 - is_head)
    shifts = range(-3, 4)
    same = {d: jnp.where(ids == ahead(ids, d), 1.0, 0.0) for d in shifts}
    norm_sq = sum(same[d] * ahead(tail * tail, d) for d in shifts)
    head_value = sum(same[d] * ahead(point * is_head, d) for d in shifts)
    norm = jnp.sqrt(jnp.where(second > 0.5, norm_sq, 1.0))
    ratio = head_value / norm
    unit = tail / norm
    positive = jnp.where(point > 0, 1.0, 0.0)
    out = {}
    for d in shifts:
        eye = 1.0 if d == 0 else 0.0
        other_unit, other_head = ahead(unit, d), ahead(is_head, d)
        head_row = 0.5 * (eye + other_unit)
        tail_row = 0.5 * (unit * other_head + (1.0 + ratio) * eye - ratio * unit * other_unit)
        soc = same[d] * jnp.where(is_head > 0.5, head_row, tail_row)
        out[d] = jnp.where(second > 0.5, soc, positive * eye)
    return out


def kernel(
    sizes, omega_hbm, a_hbm, scale_hbm, point_hbm, id_hbm, kind_hbm, q_ref, r_ref,
    omega, a, scale, point, ids, kinds,
    part_out, part_in, cut, weighted, near_out, near_in, far_out, far_in,
    gram_g, gram_h,
    load_sem, a_sem, relay_sem,
    s_part, r_part, s_cut, r_cut, s_w, r_w, s_near, r_near, s_far, r_far, s_ga, r_ga, s_gb, r_gb,
):
    nx, ny, nz, nc = sizes
    np_ = ny * nc
    ng, nh = 2 * np_, nz // 2
    sketch, variables = omega.shape
    half_k, half_n = sketch // 2, variables // 2
    total = variables * ny * nz * nc
    x, y, z, c = (lax.axis_index(n) for n in ("row",) + COL)
    p = y * nc + c
    zh, zl = z // 2, lax.rem(z, 2)
    h = p * 2 + zl
    ys = [y] + [lax.rem(y + r, ny) for r in range(1, ny)]
    cs = [c, 1 - c] if nc == 2 else [c]
    zls = [zl, 1 - zl]
    zhs = [zh] + [lax.rem(zh + r, nh) for r in range(1, nh)]

    def on_g(r):
        ry, rc, rz = r
        where = {"col_0": ys[ry], "col_1": zh * 2 + zls[rz], "col_2": cs[rc]}
        return (ys[ry] * nc + cs[rc]) * 2 + zls[rz], where

    def on_h(r):
        return zhs[r], {"col_1": zhs[r] * 2 + zl}

    partners = [{"row": x + 1 - 2 * lax.rem(x, 2)}, {"row": 3 - x}] if nx == 4 else []
    y_steps = offsets_far_first(ny) + [0]
    g_steps = [(ry, rc, rz) for ry in y_steps for rc in range(nc) for rz in (1, 0) if ry or rc or rz]
    h_steps = offsets_far_first(nh)
    near_h = sorted({1, nh - 1}) if nh > 1 else []

    barrier = pltpu.get_barrier_semaphore()
    def a_rows(k):
        return pl.ds(pl.multiple_of(k * nc * LANES, nc * LANES), nc * LANES)

    def load_a(k):
        return pltpu.make_async_copy(a_hbm.at[a_rows(k), :], a.at[a_rows(k), :], a_sem.at[k])

    loads = [
        pltpu.make_async_copy(src, dst, load_sem.at[k])
        for k, (src, dst) in enumerate(
            ((omega_hbm, omega), (scale_hbm, scale), (point_hbm, point), (id_hbm, ids), (kind_hbm, kinds))
        )
    ]
    for copy in loads[:2]:
        copy.start()
    for r in y_steps:
        load_a(ys[r]).start()
    for copy in loads[2:]:
        copy.start()
    greet = [on_g(r)[1] for r in g_steps] + [on_h(r)[1] for r in near_h] + partners
    for where in greet:
        pl.semaphore_signal(barrier, inc=1, device_id=where, device_id_type=MESH)


    def send(src, dst, ss, rs, where):
        copy = pltpu.make_async_remote_copy(
            src_ref=src, dst_ref=dst, send_sem=ss, recv_sem=rs, device_id=where, device_id_type=MESH
        )
        copy.start()
        return copy

    def arrive(dst, ss, rs, where):
        pltpu.make_async_remote_copy(
            src_ref=dst, dst_ref=dst, send_sem=ss, recv_sem=rs, device_id=where, device_id_type=MESH
        ).wait_recv()

    def drain(copies):
        for copy in copies:
            copy.wait_send()

    def sketch_part(scaled, k):
        return lax.dot_general(scaled, a[a_rows(k), :], NT, preferred_element_type=jnp.float32)

    def add_up(ref, g, count, piece=(0, half_k)):
        lo, hi = piece[0], piece[0] + piece[1]
        out = ref[g, 0, lo:hi].astype(jnp.float32)
        for t in range(1, count):
            out = out + ref[g, t, lo:hi].astype(jnp.float32)
        return out

    def gram_start(g, rows):
        rows = rows.astype(jnp.bfloat16)
        local = lax.dot_general(rows, rows, NT, preferred_element_type=jnp.float32)
        gram_g[g, h] = packed(local).astype(jnp.bfloat16)
        out = []
        for r in g_steps:
            k, where = on_g(r)
            out.append(send(gram_g.at[g, h], gram_g.at[g, h], s_ga.at[g, k], r_ga.at[g, h], where))
        return out

    def gram_cross(g):
        for r in g_steps:
            k, where = on_g(r)
            arrive(gram_g.at[g, k], s_ga.at[g, k], r_ga.at[g, k], where)
        gram_h[g, zh] = add_up(gram_g, g, ng).astype(jnp.bfloat16)
        out = []
        for r in h_steps:
            k, where = on_h(r)
            out.append(send(gram_h.at[g, zh], gram_h.at[g, zh], s_gb.at[g, r], r_gb.at[g, zh], where))
        return out

    def gram_collect(g):
        for r in h_steps[::-1]:
            k, where = on_h(r)
            arrive(gram_h.at[g, k], s_gb.at[g, r], r_gb.at[g, k], where)
        return Factor(unpacked(add_up(gram_h, g, nh) / total))

    relays = []
    known = 1
    while known < nh // 2:
        relays.append(known)
        known *= 2

    def relay_signal(step):
        for side, r in enumerate((relays[step], nh - relays[step])):
            pl.semaphore_signal(relay_sem.at[step, side], inc=1, device_id=on_h(r)[1], device_id_type=MESH)

    def relay_wait(step):
        for side in range(2):
            pl.semaphore_wait(relay_sem.at[step, side], 1)

    def view(ref, index, piece):
        return ref.at[(*index, pl.ds(piece[0], piece[1]))]

    count = len(PIECES)

    def store_part(g, k, part, pieces):
        for e in range(nc):
            at = 0
            for lo, n in pieces:
                for t in range(2):
                    rows = part[at : at + n, LANES * e : LANES * (e + 1)]
                    part_out[g, k * nc + e, t, lo : lo + n] = rows.astype(jnp.bfloat16)
                    at += n

    def send_part(g, i, r):
        out = []
        for rc in range(nc):
            for rz in (1, 0):
                if r or rc or rz:
                    to, where = on_g((r, rc, rz))
                    out.append(
                        send(
                            view(part_out, (g, ys[r] * nc + cs[rc], zls[rz]), PIECES[i]),
                            view(part_in, (g, h), PIECES[i]),
                            s_part.at[g, i, to], r_part.at[g, i, h], where,
                        )
                    )
        return out

    def own_rows(part, at, n):
        mine = jnp.where(c == 0, part[at : at + 2 * n, :LANES], part[at : at + 2 * n, -LANES:])
        return jnp.where(zl == 0, mine[:n], mine[n:])

    for copy in loads[:2]:
        copy.wait()
    scaled = (omega[...].astype(jnp.float32) * scale[...]).astype(jnp.bfloat16)
    scaled = jnp.concatenate(
        [scaled[half_k * t + lo : half_k * t + lo + n] for lo, n in PIECES for t in range(2)], axis=0
    )
    sends, owned = [], []
    for r in y_steps:
        load_a(ys[r]).wait()
        part = sketch_part(scaled, ys[r])
        store_part(0, ys[r], part, PIECES)
    at = 0
    for lo, n in PIECES:
        owned.append(own_rows(part, at, n))
        at += 2 * n
    pl.semaphore_wait(barrier, len(greet))
    if relays:
        relay_signal(0)
    for i in range(count):
        for r in y_steps:
            sends += send_part(0, i, r)
    for step in range(len(relays)):
        relay_wait(step)
        if step + 1 < len(relays):
            relay_signal(step + 1)
    for copy in loads[2:]:
        copy.wait()
    coef = cone_coefficients(point[pl.ds(p, 1), :], ids[pl.ds(p, 1), :], kinds[pl.ds(p, 1), :])
    gram_sends, late = [], []
    for g in range(PASSES):
        cut_sends = []
        for i, piece in enumerate(PIECES):
            lo, n = piece
            mine = owned[i]
            for r in g_steps:
                k, where = on_g(r)
                arrive(view(part_in, (g, k), piece), s_part.at[g, i, k], r_part.at[g, i, k], where)
                mine = mine + part_in[g, k, lo : lo + n].astype(jnp.float32)
            cut[g, zh, lo : lo + n] = mine.astype(jnp.bfloat16)
            for r in h_steps:
                k, where = on_h(r)
                cut_sends.append(
                    send(
                        view(cut, (g, zh), piece), view(cut, (g, zh), piece),
                        s_cut.at[g, i, r], r_cut.at[g, i, zh], where,
                    )
                )
        drain(sends)
        drain(late)
        if g == 1:
            gram_sends += gram_cross(0)
        w_sends = []
        for i, piece in enumerate(PIECES):
            lo, n = piece
            for r in h_steps[::-1]:
                k, where = on_h(r)
                arrive(view(cut, (g, k), piece), s_cut.at[g, i, r], r_cut.at[g, i, k], where)
            mine = add_up(cut, g, nh, piece)
            shaped = sum(coef[d] * (mine if d == 0 else pltpu.roll(mine, (-d) % LANES, 1)) for d in range(-3, 4))
            weighted[g, h, lo : lo + n] = shaped.astype(jnp.bfloat16)
            for r in g_steps:
                k, where = on_g(r)
                w_sends.append(
                    send(
                        view(weighted, (g, h), piece), view(weighted, (g, h), piece),
                        s_w.at[g, i, k], r_w.at[g, i, h], where,
                    )
                )
        drain(cut_sends)
        near_sends, far_sends = [], []
        for i, piece in enumerate(PIECES):
            lo, n = piece
            for r in g_steps:
                k, where = on_g(r)
                arrive(view(weighted, (g, k), piece), s_w.at[g, i, k], r_w.at[g, i, k], where)
            whole = jnp.concatenate(
                [
                    jnp.concatenate([weighted[g, 2 * t, lo : lo + n], weighted[g, 2 * t + 1, lo : lo + n]], axis=0)
                    for t in range(np_)
                ],
                axis=1,
            )
            for t in range(2):
                back = jnp.dot(whole, a[:, half_n * t : half_n * (t + 1)], preferred_element_type=jnp.float32)
                near_out[g, t, 2 * lo : 2 * (lo + n)] = back.astype(jnp.bfloat16)
                if partners:
                    double = (2 * lo, 2 * n)
                    near_sends.append(
                        send(
                            view(near_out, (g, t), double), view(near_in, (g, t), double),
                            s_near.at[g, i, t], r_near.at[g, i, t], partners[t],
                        )
                    )
        drain(w_sends)
        if g == 1:
            factor = gram_collect(0)
            factor.run(0, 24)
        for i, piece in enumerate(PIECES if partners else ()):
            double = (2 * piece[0], 2 * piece[1])
            lo, hi = double[0], double[0] + double[1]
            for t in range(2):
                arrive(view(near_in, (g, t), double), s_near.at[g, i, t], r_near.at[g, i, t], partners[t])
                pair = near_out[g, t, lo:hi].astype(jnp.float32) + near_in[g, t, lo:hi].astype(jnp.float32)
                far_out[g, t, lo:hi] = pair.astype(jnp.bfloat16)
                far_sends.append(
                    send(
                        view(far_out, (g, t), double), view(far_in, (g, t), double),
                        s_far.at[g, i, t], r_far.at[g, i, t], partners[1 - t],
                    )
                )
            if g == 1 and i == 0:
                factor.run(24, half_k)
        if g == 1:
            factor.run(half_k, sketch)
            drain(gram_sends)
        late = near_sends + far_sends
        summed, owned, sends = [], [], []
        for i, piece in enumerate(PIECES):
            double = (2 * piece[0], 2 * piece[1])
            lo, hi = double[0], double[0] + double[1]
            halves = []
            for t in range(2):
                if partners:
                    arrive(view(far_in, (g, t), double), s_far.at[g, i, t], r_far.at[g, i, t], partners[1 - t])
                    halves.append(far_out[g, t, lo:hi].astype(jnp.float32) + far_in[g, t, lo:hi].astype(jnp.float32))
                else:
                    halves.append(near_out[g, t, lo:hi].astype(jnp.float32))
            rows = jnp.concatenate(halves, axis=1) * scale[...]
            summed.append(rows)
            if g == 0:
                scaled = (rows * scale[...]).astype(jnp.bfloat16)
                for r in y_steps:
                    part = sketch_part(scaled, ys[r])
                    store_part(1, ys[r], part, (piece,))
                    sends += send_part(1, i, r)
                owned.append(own_rows(part, 0, piece[1]))
        summed = jnp.concatenate([v[n * t : n * (t + 1)] for t in range(2) for v, (_, n) in zip(summed, PIECES)], axis=0)
        if g == 0:
            gram_sends += gram_start(0, summed)
        else:
            _, inverse = factor.result()
            final = split_dot(inverse[:, :sketch], summed)
            sends = gram_start(1, final)
            drain(late)
            sends += gram_cross(1)
            factor = gram_collect(1)
            factor.run(0, sketch)
            upper, inverse = factor.result()
            q_ref[...] = split_dot(inverse[:, :sketch], final)
            r_ref[...] = upper[:, :sketch]
            drain(sends)


def local(a_matrix, omega, col_scale, cone_point, cone_id, cone_kind):
    sketch, variables = omega.shape
    rows = a_matrix.shape[0]
    nx, ny, nz, nc = (lax.axis_size(n) for n in ("row",) + COL)
    np_ = ny * nc
    ng, nh = 2 * np_, nz // 2
    g = PASSES
    bf, f32, i32 = jnp.bfloat16, jnp.float32, jnp.int32
    dma = pltpu.SemaphoreType.DMA
    any_spec = pl.BlockSpec(memory_space=pl.ANY)
    vmem_spec = pl.BlockSpec(memory_space=pltpu.VMEM)
    n = len(PIECES)
    per_g, per_h, per_x = dma((g, n, ng)), dma((g, n, nh)), dma((g, n, 2))
    gram_by_g, gram_by_h = dma((g, ng)), dma((g, nh))
    cross = pltpu.VMEM((g, 2, sketch, variables // 2), bf)

    def body(*refs):
        kernel((nx, ny, nz, nc), *refs)

    return tuple(
        pl.pallas_call(
            body,
            out_shape=(
                jax.ShapeDtypeStruct((sketch, variables), f32),
                jax.ShapeDtypeStruct((sketch, sketch), f32),
            ),
            in_specs=[any_spec] * 6,
            out_specs=(vmem_spec, vmem_spec),
            scratch_shapes=[
                pltpu.VMEM((sketch, variables), bf),
                pltpu.VMEM((rows, variables), bf),
                pltpu.VMEM((1, variables), f32),
                pltpu.VMEM((np_, LANES), f32),
                pltpu.VMEM((np_, LANES), i32),
                pltpu.VMEM((np_, LANES), i32),
                pltpu.VMEM((g, np_, 2, sketch // 2, LANES), bf),
                pltpu.VMEM((g, ng, sketch // 2, LANES), bf),
                pltpu.VMEM((g, nh, sketch // 2, LANES), bf),
                pltpu.VMEM((g, ng, sketch // 2, LANES), bf),
                cross, cross, cross, cross,
                pltpu.VMEM((g, ng, sketch // 2, LANES), bf),
                pltpu.VMEM((g, nh, sketch // 2, LANES), bf),
                dma((5,)),
                dma((ny,)),
                pltpu.SemaphoreType.REGULAR((3, 2)),
                per_g, per_g, per_h, per_h, per_g, per_g, per_x, per_x, per_x, per_x,
                gram_by_g, gram_by_g, gram_by_h, gram_by_h,
            ],
            compiler_params=pltpu.CompilerParams(collective_id=0, has_side_effects=True),
        )(
            omega,
            a_matrix,
            col_scale.reshape(1, variables),
            cone_point.reshape(np_, LANES),
            cone_id.reshape(np_, LANES),
            cone_kind.reshape(np_, LANES),
        )
    )


def solution(mesh):
    shape = mesh.shape
    parts = (4, 16, 2) if shape["col"] == 128 else (1, shape["col"], 1)
    split = Mesh(mesh.devices.reshape(shape["row"], *parts), ("row",) + COL)
    in_specs = (P("row", COL), P(None, COL), P(COL), P("row"), P("row"), P("row"))
    out_specs = (P(None, COL), P())
    return jax.shard_map(local, mesh=split, in_specs=in_specs, out_specs=out_specs, check_vma=False)
```

```python
import jax
import jax.numpy as jnp
from jax import lax
from jax.experimental import pallas as pl
from jax.experimental.pallas import tpu as pltpu
from jax.sharding import Mesh
from jax.sharding import PartitionSpec as P

PASSES = 2
PIECES = ((0, 16), (16, 32))
LANES = 128
SUB = 8
COL = ("col_0", "col_1", "col_2")
MESH = pl.DeviceIdType.MESH
NT = (((1,), (1,)), ((), ()))


def offsets_far_first(n):
    return sorted(range(1, n), key=lambda r: -min(r, n - r))


def iota(dim, shape=(SUB, LANES)):
    return lax.broadcasted_iota(jnp.int32, shape, dim)


class Factor:
    STEP = 8

    def __init__(self, gram):
        self.n = n = gram.shape[0]
        self.blocks = n // SUB
        self.m = [gram[SUB * i : SUB * (i + 1)] for i in range(self.blocks)]
        self.upper = [jnp.zeros((SUB, LANES), jnp.float32) for _ in range(self.blocks)]
        self.inverse = [jnp.zeros((SUB, LANES), jnp.float32) for _ in range(self.blocks)]

    def run(self, first, last):
        m, upper, inverse, blocks, step = self.m, self.upper, self.inverse, self.blocks, self.STEP
        lane, row = iota(1), iota(0)

        def down(block, s):
            return jnp.broadcast_to(block[s : s + 1, :], (SUB, LANES))

        for j in range(first, last, step):
            jb, s0 = j // SUB, j % SUB
            cols = [
                {i: jnp.broadcast_to(m[i][:, j + t : j + t + 1], (SUB, LANES)) for i in range(jb, blocks)}
                for t in range(step)
            ]
            rows = [down(m[jb], s0 + t) for t in range(step)]
            mults, pivots = [], []
            for t in range(step):
                d = down(cols[t][jb], s0 + t)
                inv = 1.0 / d
                root = lax.rsqrt(d)
                at = row == s0 + t
                here = lane == j + t
                upper[jb] = jnp.where(at & (lane >= j + t), rows[t] * root, upper[jb])
                inverse[jb] = jnp.where(at & (lane < j + t), rows[t] * root, jnp.where(at & here, root, inverse[jb]))
                mult = {i: cols[t][i] * inv for i in cols[t]}
                pivot = jnp.where(here, 1.0, rows[t])
                for u in range(t + 1, step):
                    head = down(cols[t][jb], s0 + u)
                    rows[u] = jnp.where(here, 0.0, rows[u]) - head * inv * pivot
                    cols[u] = {i: cols[u][i] - mult[i] * head for i in cols[u]}
                mults.append(mult)
                pivots.append(jnp.where((lane > j + t) & (lane < j + step), 0.0, pivot))
            inside = (lane >= j) & (lane < j + step)
            for i in range(jb, blocks):
                if i == jb and s0 + step == SUB:
                    continue
                new = jnp.where(inside, 0.0, m[i])
                for t in range(step):
                    new = new - mults[t][i] * pivots[t]
                m[i] = jnp.where(row >= s0 + step, new, m[i]) if i == jb else new

    def result(self):
        return jnp.concatenate(self.upper, axis=0), jnp.concatenate(self.inverse, axis=0)


def split_dot(left, right):
    f32, bf = jnp.float32, jnp.bfloat16
    lh, rh = left.astype(bf), right.astype(bf)
    ll, rl = (left - lh.astype(f32)).astype(bf), (right - rh.astype(f32)).astype(bf)
    small = jnp.dot(ll, rh, preferred_element_type=f32) + jnp.dot(lh, rl, preferred_element_type=f32)
    return jnp.dot(lh, rh, preferred_element_type=f32) + small


def packed(gram):
    n = gram.shape[0]
    wide = jnp.concatenate([gram, jnp.zeros((n, LANES - n), jnp.float32)], axis=1)
    tiles = [wide[SUB * i : SUB * (i + 1)] for i in range(n // SUB)]
    lane = iota(1)
    out = []
    for i in range(n // SUB // 2):
        cut = SUB * (i + 1)
        out.append(jnp.where(lane < cut, tiles[i], pltpu.roll(tiles[-1 - i], cut, 1)))
    return jnp.concatenate(out, axis=0)


def unpacked(half):
    count = half.shape[0] // SUB
    lane = iota(1)
    low, high = [], []
    for i in range(count):
        tile = half[SUB * i : SUB * (i + 1)]
        cut = SUB * (i + 1)
        low.append(jnp.where(lane < cut, tile, 0.0))
        high.append(jnp.where(lane < SUB * (2 * count - i), pltpu.roll(tile, LANES - cut, 1), 0.0))
    n = 2 * count * SUB
    lower = jnp.concatenate(low + high[::-1] + [jnp.zeros((LANES - n, LANES), jnp.float32)], axis=0)
    row, col = iota(0, (LANES, LANES)), iota(1, (LANES, LANES))
    return jnp.where(col // SUB > row // SUB, lower.T, lower)[:n]


def cone_coefficients(point, ids, kinds):
    width = point.shape[1]

    def ahead(v, d):
        return v if d == 0 else pltpu.roll(v, (-d) % width, 1)

    is_head = jnp.where(ids != ahead(ids, -1), 1.0, 0.0)
    second = jnp.where(kinds == 1, 1.0, 0.0)
    tail = point * second * (1.0 - is_head)
    shifts = range(-3, 4)
    same = {d: jnp.where(ids == ahead(ids, d), 1.0, 0.0) for d in shifts}
    norm_sq = sum(same[d] * ahead(tail * tail, d) for d in shifts)
    head_value = sum(same[d] * ahead(point * is_head, d) for d in shifts)
    norm = jnp.sqrt(jnp.where(second > 0.5, norm_sq, 1.0))
    ratio = head_value / norm
    unit = tail / norm
    positive = jnp.where(point > 0, 1.0, 0.0)
    out = {}
    for d in shifts:
        eye = 1.0 if d == 0 else 0.0
        other_unit, other_head = ahead(unit, d), ahead(is_head, d)
        head_row = 0.5 * (eye + other_unit)
        tail_row = 0.5 * (unit * other_head + (1.0 + ratio) * eye - ratio * unit * other_unit)
        soc = same[d] * jnp.where(is_head > 0.5, head_row, tail_row)
        out[d] = jnp.where(second > 0.5, soc, positive * eye)
    return out


def kernel(
    sizes, omega_hbm, a_hbm, scale_hbm, point_hbm, id_hbm, kind_hbm, q_ref, r_ref,
    omega, a, scale, point, ids, kinds,
    part_out, part_in, cut, weighted, near_out, near_in, far_out, far_in,
    gram_g, gram_h,
    load_sem, a_sem, relay_sem,
    s_part, r_part, s_cut, r_cut, s_w, r_w, s_near, r_near, s_far, r_far, s_ga, r_ga, s_gb, r_gb,
):
    nx, ny, nz, nc = sizes
    np_ = ny * nc
    ng, nh = 2 * np_, nz // 2
    sketch, variables = omega.shape
    half_k, half_n = sketch // 2, variables // 2
    total = variables * ny * nz * nc
    x, y, z, c = (lax.axis_index(n) for n in ("row",) + COL)
    p = y * nc + c
    zh, zl = z // 2, lax.rem(z, 2)
    h = p * 2 + zl
    ys = [y] + [lax.rem(y + r, ny) for r in range(1, ny)]
    cs = [c, 1 - c] if nc == 2 else [c]
    zls = [zl, 1 - zl]
    zhs = [zh] + [lax.rem(zh + r, nh) for r in range(1, nh)]

    def on_g(r):
        ry, rc, rz = r
        where = {"col_0": ys[ry], "col_1": zh * 2 + zls[rz], "col_2": cs[rc]}
        return (ys[ry] * nc + cs[rc]) * 2 + zls[rz], where

    def on_h(r):
        return zhs[r], {"col_1": zhs[r] * 2 + zl}

    partners = [{"row": x + 1 - 2 * lax.rem(x, 2)}, {"row": 3 - x}] if nx == 4 else []
    y_steps = offsets_far_first(ny) + [0]
    g_steps = [(ry, rc, rz) for ry in y_steps for rc in range(nc) for rz in (1, 0) if ry or rc or rz]
    h_steps = offsets_far_first(nh)
    near_h = sorted({1, nh - 1}) if nh > 1 else []

    barrier = pltpu.get_barrier_semaphore()
    def a_rows(k):
        return pl.ds(pl.multiple_of(k * nc * LANES, nc * LANES), nc * LANES)

    def load_a(k):
        return pltpu.make_async_copy(a_hbm.at[a_rows(k), :], a.at[a_rows(k), :], a_sem.at[k])

    loads = [
        pltpu.make_async_copy(src, dst, load_sem.at[k])
        for k, (src, dst) in enumerate(
            ((omega_hbm, omega), (scale_hbm, scale), (point_hbm, point), (id_hbm, ids), (kind_hbm, kinds))
        )
    ]
    for copy in loads[:2]:
        copy.start()
    for r in y_steps:
        load_a(ys[r]).start()
    for copy in loads[2:]:
        copy.start()
    greet = [on_g(r)[1] for r in g_steps] + [on_h(r)[1] for r in near_h] + partners
    for where in greet:
        pl.semaphore_signal(barrier, inc=1, device_id=where, device_id_type=MESH)


    def send(src, dst, ss, rs, where):
        copy = pltpu.make_async_remote_copy(
            src_ref=src, dst_ref=dst, send_sem=ss, recv_sem=rs, device_id=where, device_id_type=MESH
        )
        copy.start()
        return copy

    def arrive(dst, ss, rs, where):
        pltpu.make_async_remote_copy(
            src_ref=dst, dst_ref=dst, send_sem=ss, recv_sem=rs, device_id=where, device_id_type=MESH
        ).wait_recv()

    def drain(copies):
        for copy in copies:
            copy.wait_send()

    def sketch_part(scaled, k):
        return lax.dot_general(scaled, a[a_rows(k), :], NT, preferred_element_type=jnp.float32)

    def add_up(ref, g, count, piece=(0, half_k)):
        lo, hi = piece[0], piece[0] + piece[1]
        out = ref[g, 0, lo:hi].astype(jnp.float32)
        for t in range(1, count):
            out = out + ref[g, t, lo:hi].astype(jnp.float32)
        return out

    def gram_start(g, rows):
        rows = rows.astype(jnp.bfloat16)
        local = lax.dot_general(rows, rows, NT, preferred_element_type=jnp.float32)
        gram_g[g, h] = packed(local).astype(jnp.bfloat16)
        out = []
        for r in g_steps:
            k, where = on_g(r)
            out.append(send(gram_g.at[g, h], gram_g.at[g, h], s_ga.at[g, k], r_ga.at[g, h], where))
        return out

    def gram_cross(g):
        for r in g_steps:
            k, where = on_g(r)
            arrive(gram_g.at[g, k], s_ga.at[g, k], r_ga.at[g, k], where)
        gram_h[g, zh] = add_up(gram_g, g, ng).astype(jnp.bfloat16)
        out = []
        for r in h_steps:
            k, where = on_h(r)
            out.append(send(gram_h.at[g, zh], gram_h.at[g, zh], s_gb.at[g, r], r_gb.at[g, zh], where))
        return out

    def gram_collect(g):
        for r in h_steps[::-1]:
            k, where = on_h(r)
            arrive(gram_h.at[g, k], s_gb.at[g, r], r_gb.at[g, k], where)
        return Factor(unpacked(add_up(gram_h, g, nh) / total))

    relays = []
    known = 1
    while known < nh // 2:
        relays.append(known)
        known *= 2

    def relay_signal(step):
        for side, r in enumerate((relays[step], nh - relays[step])):
            pl.semaphore_signal(relay_sem.at[step, side], inc=1, device_id=on_h(r)[1], device_id_type=MESH)

    def relay_wait(step):
        for side in range(2):
            pl.semaphore_wait(relay_sem.at[step, side], 1)

    def view(ref, index, piece):
        return ref.at[(*index, pl.ds(piece[0], piece[1]))]

    count = len(PIECES)

    def store_part(g, k, part, pieces):
        for e in range(nc):
            at = 0
            for lo, n in pieces:
                for t in range(2):
                    rows = part[at : at + n, LANES * e : LANES * (e + 1)]
                    part_out[g, k * nc + e, t, lo : lo + n] = rows.astype(jnp.bfloat16)
                    at += n

    def send_part(g, i, r):
        out = []
        for rc in range(nc):
            for rz in (1, 0):
                if r or rc or rz:
                    to, where = on_g((r, rc, rz))
                    out.append(
                        send(
                            view(part_out, (g, ys[r] * nc + cs[rc], zls[rz]), PIECES[i]),
                            view(part_in, (g, h), PIECES[i]),
                            s_part.at[g, i, to], r_part.at[g, i, h], where,
                        )
                    )
        return out

    def own_rows(part, at, n):
        mine = jnp.where(c == 0, part[at : at + 2 * n, :LANES], part[at : at + 2 * n, -LANES:])
        return jnp.where(zl == 0, mine[:n], mine[n:])

    for copy in loads[:2]:
        copy.wait()
    scaled = (omega[...].astype(jnp.float32) * scale[...]).astype(jnp.bfloat16)
    scaled = jnp.concatenate(
        [scaled[half_k * t + lo : half_k * t + lo + n] for lo, n in PIECES for t in range(2)], axis=0
    )
    sends, owned = [], []
    for r in y_steps:
        load_a(ys[r]).wait()
        part = sketch_part(scaled, ys[r])
        store_part(0, ys[r], part, PIECES)
    at = 0
    for lo, n in PIECES:
        owned.append(own_rows(part, at, n))
        at += 2 * n
    pl.semaphore_wait(barrier, len(greet))
    if relays:
        relay_signal(0)
    for i in range(count):
        for r in y_steps:
            sends += send_part(0, i, r)
    for step in range(len(relays)):
        relay_wait(step)
        if step + 1 < len(relays):
            relay_signal(step + 1)
    for copy in loads[2:]:
        copy.wait()
    coef = cone_coefficients(point[pl.ds(p, 1), :], ids[pl.ds(p, 1), :], kinds[pl.ds(p, 1), :])
    gram_sends, late = [], []
    for g in range(PASSES):
        cut_sends = []
        for i, piece in enumerate(PIECES):
            lo, n = piece
            mine = owned[i]
            for r in g_steps:
                k, where = on_g(r)
                arrive(view(part_in, (g, k), piece), s_part.at[g, i, k], r_part.at[g, i, k], where)
                mine = mine + part_in[g, k, lo : lo + n].astype(jnp.float32)
            cut[g, zh, lo : lo + n] = mine.astype(jnp.bfloat16)
            for r in h_steps:
                k, where = on_h(r)
                cut_sends.append(
                    send(
                        view(cut, (g, zh), piece), view(cut, (g, zh), piece),
                        s_cut.at[g, i, r], r_cut.at[g, i, zh], where,
                    )
                )
        drain(sends)
        drain(late)
        if g == 1:
            gram_sends += gram_cross(0)
        w_sends = []
        for i, piece in enumerate(PIECES):
            lo, n = piece
            for r in h_steps[::-1]:
                k, where = on_h(r)
                arrive(view(cut, (g, k), piece), s_cut.at[g, i, r], r_cut.at[g, i, k], where)
            mine = add_up(cut, g, nh, piece)
            shaped = sum(coef[d] * (mine if d == 0 else pltpu.roll(mine, (-d) % LANES, 1)) for d in range(-3, 4))
            weighted[g, h, lo : lo + n] = shaped.astype(jnp.bfloat16)
            for r in g_steps:
                k, where = on_g(r)
                w_sends.append(
                    send(
                        view(weighted, (g, h), piece), view(weighted, (g, h), piece),
                        s_w.at[g, i, k], r_w.at[g, i, h], where,
                    )
                )
        drain(cut_sends)
        near_sends, far_sends = [], []
        for i, piece in enumerate(PIECES):
            lo, n = piece
            for r in g_steps:
                k, where = on_g(r)
                arrive(view(weighted, (g, k), piece), s_w.at[g, i, k], r_w.at[g, i, k], where)
            whole = jnp.concatenate(
                [
                    jnp.concatenate([weighted[g, 2 * t, lo : lo + n], weighted[g, 2 * t + 1, lo : lo + n]], axis=0)
                    for t in range(np_)
                ],
                axis=1,
            )
            for t in range(2):
                back = jnp.dot(whole, a[:, half_n * t : half_n * (t + 1)], preferred_element_type=jnp.float32)
                near_out[g, t, 2 * lo : 2 * (lo + n)] = back.astype(jnp.bfloat16)
                if partners:
                    double = (2 * lo, 2 * n)
                    near_sends.append(
                        send(
                            view(near_out, (g, t), double), view(near_in, (g, t), double),
                            s_near.at[g, i, t], r_near.at[g, i, t], partners[t],
                        )
                    )
        drain(w_sends)
        if g == 1:
            factor = gram_collect(0)
            factor.run(0, 24)
        for i, piece in enumerate(PIECES if partners else ()):
            double = (2 * piece[0], 2 * piece[1])
            lo, hi = double[0], double[0] + double[1]
            for t in range(2):
                arrive(view(near_in, (g, t), double), s_near.at[g, i, t], r_near.at[g, i, t], partners[t])
                pair = near_out[g, t, lo:hi].astype(jnp.float32) + near_in[g, t, lo:hi].astype(jnp.float32)
                far_out[g, t, lo:hi] = pair.astype(jnp.bfloat16)
                far_sends.append(
                    send(
                        view(far_out, (g, t), double), view(far_in, (g, t), double),
                        s_far.at[g, i, t], r_far.at[g, i, t], partners[1 - t],
                    )
                )
            if g == 1 and i == 0:
                factor.run(24, half_k)
        if g == 1:
            factor.run(half_k, sketch)
            drain(gram_sends)
        late = near_sends + far_sends
        summed, owned, sends = [], [], []
        for i, piece in enumerate(PIECES):
            double = (2 * piece[0], 2 * piece[1])
            lo, hi = double[0], double[0] + double[1]
            halves = []
            for t in range(2):
                if partners:
                    arrive(view(far_in, (g, t), double), s_far.at[g, i, t], r_far.at[g, i, t], partners[1 - t])
                    halves.append(far_out[g, t, lo:hi].astype(jnp.float32) + far_in[g, t, lo:hi].astype(jnp.float32))
                else:
                    halves.append(near_out[g, t, lo:hi].astype(jnp.float32))
            rows = jnp.concatenate(halves, axis=1) * scale[...]
            summed.append(rows)
            if g == 0:
                scaled = (rows * scale[...]).astype(jnp.bfloat16)
                for r in y_steps:
                    part = sketch_part(scaled, ys[r])
                    store_part(1, ys[r], part, (piece,))
                    sends += send_part(1, i, r)
                owned.append(own_rows(part, 0, piece[1]))
        summed = jnp.concatenate([v[n * t : n * (t + 1)] for t in range(2) for v, (_, n) in zip(summed, PIECES)], axis=0)
        if g == 0:
            gram_sends += gram_start(0, summed)
        else:
            _, inverse = factor.result()
            final = split_dot(inverse[:, :sketch], summed)
            sends = gram_start(1, final)
            drain(late)
            sends += gram_cross(1)
            factor = gram_collect(1)
            factor.run(0, sketch)
            upper, inverse = factor.result()
            q_ref[...] = split_dot(inverse[:, :sketch], final)
            r_ref[...] = upper[:, :sketch]
            drain(sends)


def local(a_matrix, omega, col_scale, cone_point, cone_id, cone_kind):
    sketch, variables = omega.shape
    rows = a_matrix.shape[0]
    nx, ny, nz, nc = (lax.axis_size(n) for n in ("row",) + COL)
    np_ = ny * nc
    ng, nh = 2 * np_, nz // 2
    g = PASSES
    bf, f32, i32 = jnp.bfloat16, jnp.float32, jnp.int32
    dma = pltpu.SemaphoreType.DMA
    any_spec = pl.BlockSpec(memory_space=pl.ANY)
    vmem_spec = pl.BlockSpec(memory_space=pltpu.VMEM)
    n = len(PIECES)
    per_g, per_h, per_x = dma((g, n, ng)), dma((g, n, nh)), dma((g, n, 2))
    gram_by_g, gram_by_h = dma((g, ng)), dma((g, nh))
    cross = pltpu.VMEM((g, 2, sketch, variables // 2), bf)

    def body(*refs):
        kernel((nx, ny, nz, nc), *refs)

    return tuple(
        pl.pallas_call(
            body,
            out_shape=(
                pltpu.VMEM((sketch, variables), f32),
                pltpu.VMEM((sketch, sketch), f32),
            ),
            in_specs=[any_spec] * 6,
            out_specs=(vmem_spec, vmem_spec),
            scratch_shapes=[
                pltpu.VMEM((sketch, variables), bf),
                pltpu.VMEM((rows, variables), bf),
                pltpu.VMEM((1, variables), f32),
                pltpu.VMEM((np_, LANES), f32),
                pltpu.VMEM((np_, LANES), i32),
                pltpu.VMEM((np_, LANES), i32),
                pltpu.VMEM((g, np_, 2, sketch // 2, LANES), bf),
                pltpu.VMEM((g, ng, sketch // 2, LANES), bf),
                pltpu.VMEM((g, nh, sketch // 2, LANES), bf),
                pltpu.VMEM((g, ng, sketch // 2, LANES), bf),
                cross, cross, cross, cross,
                pltpu.VMEM((g, ng, sketch // 2, LANES), bf),
                pltpu.VMEM((g, nh, sketch // 2, LANES), bf),
                dma((5,)),
                dma((ny,)),
                pltpu.SemaphoreType.REGULAR((3, 2)),
                per_g, per_g, per_h, per_h, per_g, per_g, per_x, per_x, per_x, per_x,
                gram_by_g, gram_by_g, gram_by_h, gram_by_h,
            ],
            compiler_params=pltpu.CompilerParams(collective_id=0, has_side_effects=True),
        )(
            omega,
            a_matrix,
            col_scale.reshape(1, variables),
            cone_point.reshape(np_, LANES),
            cone_id.reshape(np_, LANES),
            cone_kind.reshape(np_, LANES),
        )
    )


def solution(mesh):
    shape = mesh.shape
    parts = (4, 16, 2) if shape["col"] == 128 else (1, shape["col"], 1)
    split = Mesh(mesh.devices.reshape(shape["row"], *parts), ("row",) + COL)
    in_specs = (P("row", COL), P(None, COL), P(COL), P("row"), P("row"), P("row"))
    out_specs = (P(None, COL), P())
    return jax.shard_map(local, mesh=split, in_specs=in_specs, out_specs=out_specs, check_vma=False)
```
